512 devices in a mesh: section: 8 (over x, core), dp: 64 (over z, y).
Axes of the slice: x: 4, y: 8, z: 8, core: 2. Of those that a mesh axis runs over, the one named last changes fastest.
Arguments:
- inputs: bfloat16 [8, 1024, 4096], P(None, 'dp')
- cotangent: bfloat16 [8, 1024, 4096], P(None, 'dp'), may hold values from -0.59765625 to 0.59765625
- row_adapter_slot: int32 [8, 1024], P(None, 'dp'), may hold values from 0 to 1
- deployed_adapter_ids: int32 [64, 2], replicated, may hold values from 0 to 63, as said below
- adapter_owner_device: int32 [64], replicated, may hold values from 0 to 63, each once
- adapter_down_weight: bfloat16 [8, 1, 64, 2, 32, 4096], P('section', None, 'dp'), as said below
- adapter_up_weight: bfloat16 [8, 1, 64, 2, 32, 4096], P('section', None, 'dp'), as said below
Outputs:
- grad_down: float32 [8, 1, 64, 32, 4096], P('section', None, 'dp')
- grad_up: float32 [8, 1, 64, 32, 4096], P('section', None, 'dp')
The draws below stay inside these ranges and needn't reach their ends.
Inputs may be any that keep to these rules, and one draw needn't show every extreme that they name: `deployed_adapter_ids`: the 2 adapter ids of one device differ, and every adapter is deployed on at least one device; some adapters are deployed on many devices. `adapter_owner_device`: every data device owns exactly one adapter. `adapter_down_weight`: copies of the same adapter on different devices are equal. `adapter_up_weight`: copies of the same adapter on different devices are equal.
All inputs are finite; a program needn't handle non-finite values.
Results may differ from the reference program's by a relative error of at most 0.0086.
Values may be sent and summed in bfloat16 or wider, within the bound.
A program may use at most 64 MiB of HBM per device.

```python
import jax
import jax.numpy as jnp
from jax import lax

MODEL_WIDTH = 4096
ADAPTER_RANK = 32
DEPLOYED_COUNT = 2
SECTION_LAYERS = 1
MB = 8
ROWS = 16
NA = 64
TOKENS = 1024
N_SECTION = 8
N_DP = 64


def deployment(key):
    base_key = jax.random.fold_in(key, 11)
    first_key, lower_key, upper_key, label_key = jax.random.split(base_key, 4)
    first_ids = jax.random.permutation(first_key, NA)
    draw_lower = jax.random.randint(lower_key, (N_DP,), 0, NA)
    draw_upper = jax.random.randint(upper_key, (N_DP,), 0, NA)
    relabel = jax.random.permutation(label_key, NA)
    other_ids = relabel[jnp.minimum(draw_lower, draw_upper)]
    other_ids = jnp.where(other_ids == first_ids, (other_ids + 1) % NA, other_ids)
    return jnp.stack([first_ids, other_ids], axis=1).astype(jnp.int32)


def adapter_copies(key, salt_value, spread):
    deployed = deployment(key).reshape(-1)
    base_key = jax.random.fold_in(key, salt_value)

    def one_adapter(adapter_id):
        return jax.random.normal(jax.random.fold_in(base_key, adapter_id), (N_SECTION, SECTION_LAYERS, ADAPTER_RANK, MODEL_WIDTH), jnp.float32)
    adapter_table = jax.vmap(one_adapter)(deployed)
    adapter_table = adapter_table.reshape(N_DP, DEPLOYED_COUNT, N_SECTION, SECTION_LAYERS, ADAPTER_RANK, MODEL_WIDTH)
    adapter_table = jnp.transpose(adapter_table, (2, 3, 0, 1, 4, 5))
    return (adapter_table * spread).astype(jnp.bfloat16)


def draw_deployed_adapter_ids(key, part):
    return deployment(key)


def draw_adapter_down_weight(key, part):
    return adapter_copies(key, 21, MODEL_WIDTH ** (-0.5))


def draw_adapter_up_weight(key, part):
    return adapter_copies(key, 23, 1.0 / 32.0)


def draw_inputs(key, part):
    noise_key, row_key, column_key = jax.random.split(key, 3)
    value_rows = jax.random.normal(noise_key, (MB, TOKENS, MODEL_WIDTH), jnp.float32)
    row_scale = jnp.exp(jax.random.uniform(row_key, (MB, TOKENS, 1), jnp.float32, -1.15, 1.15))
    column_scale = jnp.exp(jax.random.uniform(column_key, (1, 1, MODEL_WIDTH), jnp.float32, -1.15, 1.15))
    return (value_rows * row_scale * column_scale).astype(jnp.bfloat16)


def with_ends(array, stream_key, smallest, top_value):
    extent = array.shape
    place = [jax.random.randint(jax.random.fold_in(stream_key, axis), (), 0, extent[axis]) for axis in range(len(extent))]
    array = array.at[tuple(place)].set(smallest)
    longest = extent.index(max(extent))
    place[longest] = (place[longest] + 1) % extent[longest]
    return array.at[tuple(place)].set(top_value)


def block_scale(stream_key, dims, cuts, low, largest):
    factor_of, own = 1.0, jax.random.fold_in(stream_key, 6)
    for axis_at, shards_of in cuts:
        steps = jnp.exp(jax.random.uniform(jax.random.fold_in(own, axis_at), (shards_of,), jnp.float32, low / len(cuts), largest / len(cuts)))
        factor_of = factor_of * jnp.repeat(steps, dims[axis_at] // shards_of).reshape([-1 if axis == axis_at else 1 for axis in range(len(dims))])
    return factor_of


def centred(key, extent, deviation, reach, shards=(), held_as=jnp.bfloat16):
    gain = block_scale(key, extent, shards, -0.22, 0.18) if shards else 1.0
    array = jax.random.normal(key, extent, jnp.float32) * deviation * gain
    return jnp.minimum(jnp.maximum(array, -reach), reach).astype(held_as)


def setup_inputs(seed: int = 0) -> dict:
    splits = jax.random.split(jax.random.key(seed), 8)
    return {
        "inputs": draw_inputs(jax.random.fold_in(splits[7], 71), 0),
        "cotangent": centred(splits[1], (MB, TOKENS, MODEL_WIDTH), 0.1, 0.59765625, ((1, 64),)),
        "row_adapter_slot": with_ends(jax.random.randint(splits[2], (MB, TOKENS), 0, DEPLOYED_COUNT), jax.random.fold_in(splits[2], 1), 0, DEPLOYED_COUNT - 1).astype(jnp.int32),
        "deployed_adapter_ids": draw_deployed_adapter_ids(jax.random.fold_in(splits[7], 71), 0),
        "adapter_owner_device": jax.random.permutation(splits[4], NA).astype(jnp.int32),
        "adapter_down_weight": draw_adapter_down_weight(jax.random.fold_in(splits[7], 71), 0),
        "adapter_up_weight": draw_adapter_up_weight(jax.random.fold_in(splits[7], 71), 0),
    }


adapter_scale = 0.5
epsilon = 1e-06

def slot_mask(slots):
    columns = jnp.arange(DEPLOYED_COUNT * ADAPTER_RANK, dtype=jnp.int32) // ADAPTER_RANK
    return slots[..., None] == columns

def norm_parts(hidden_state):
    value_rows = hidden_state.astype(jnp.float32)
    inverse = lax.rsqrt(lax.optimization_barrier(jnp.mean(value_rows * value_rows, axis=-1, keepdims=True)) + epsilon)
    return (value_rows, inverse, value_rows * inverse)

def forward_layer(hidden_state, down_weight, up_weight, row_mask):
    value_rows, inverse, unit = norm_parts(hidden_state)
    normed = unit.astype(jnp.bfloat16)
    rank_complete = jnp.einsum('yct,yot->yco', normed.astype(jnp.float32), down_weight.astype(jnp.float32))
    rank_row_values = jnp.where(row_mask, rank_complete, 0.0).astype(jnp.bfloat16)
    row_updates = jnp.einsum('drk,dkx->drx', rank_row_values.astype(jnp.float32), up_weight.astype(jnp.float32))
    return ((value_rows + adapter_scale * row_updates).astype(jnp.bfloat16), rank_row_values)

def backward_layer(hidden_state, rank_row_values, grad_rows, down_weight, up_weight, row_mask):
    value_rows, inverse, unit = norm_parts(hidden_state)
    normed = unit.astype(jnp.bfloat16)
    gradient_float = grad_rows.astype(jnp.float32)
    rank_complete = adapter_scale * jnp.einsum('yct,yot->yco', gradient_float, up_weight.astype(jnp.float32))
    rank_grads = jnp.where(row_mask, rank_complete, 0.0).astype(jnp.bfloat16)
    unit_grads = jnp.einsum('drk,dkx->drx', rank_grads.astype(jnp.float32), down_weight.astype(jnp.float32))
    back_rows = gradient_float + inverse * (unit_grads - unit * lax.optimization_barrier(jnp.mean(unit_grads * unit, axis=-1, keepdims=True)))
    tile_down = jnp.einsum('csg,csj->cgj', rank_grads.astype(jnp.float32), normed.astype(jnp.float32))
    up_tiled = adapter_scale * jnp.einsum('csg,csj->cgj', rank_row_values.astype(jnp.float32), gradient_float)
    return (back_rows.astype(jnp.bfloat16), tile_down, up_tiled)

def owner_sum(select, tile):
    return jnp.einsum('odk,dkrx->orx', select, tile.reshape(N_DP, DEPLOYED_COUNT, ADAPTER_RANK, MODEL_WIDTH), precision=lax.Precision.HIGHEST)

def reference(inputs, cotangent, row_adapter_slot, deployed_adapter_ids, adapter_owner_device, adapter_down_weight, adapter_up_weight):
    owner_of = adapter_owner_device[deployed_adapter_ids]
    select = (owner_of[None, :, :] == jnp.arange(NA, dtype=jnp.int32)[:, None, None]).astype(jnp.float32)
    down_weight_stack = adapter_down_weight.reshape(N_SECTION, SECTION_LAYERS, N_DP, DEPLOYED_COUNT * ADAPTER_RANK, MODEL_WIDTH)
    up_weight_stack = adapter_up_weight.reshape(N_SECTION, SECTION_LAYERS, N_DP, DEPLOYED_COUNT * ADAPTER_RANK, MODEL_WIDTH)
    grad_down = jnp.zeros((N_SECTION, SECTION_LAYERS, NA, ADAPTER_RANK, MODEL_WIDTH), jnp.float32)
    grad_up = jnp.zeros((N_SECTION, SECTION_LAYERS, NA, ADAPTER_RANK, MODEL_WIDTH), jnp.float32)
    for micro_idx in range(MB):
        row_mask = slot_mask(row_adapter_slot[micro_idx].reshape(N_DP, ROWS))
        hidden_state = inputs[micro_idx].reshape(N_DP, ROWS, MODEL_WIDTH)
        saved = []
        for section_idx in range(N_SECTION):
            for layer_idx in range(SECTION_LAYERS):
                new_hidden, rank_row_values = forward_layer(hidden_state, down_weight_stack[section_idx, layer_idx], up_weight_stack[section_idx, layer_idx], row_mask)
                saved.append((section_idx, layer_idx, hidden_state, rank_row_values))
                hidden_state = new_hidden
        grad_rows = cotangent[micro_idx].reshape(N_DP, ROWS, MODEL_WIDTH)
        for section_idx, layer_idx, hidden_state, rank_row_values in reversed(saved):
            grad_rows, tile_down, up_tiled = backward_layer(hidden_state, rank_row_values, grad_rows, down_weight_stack[section_idx, layer_idx], up_weight_stack[section_idx, layer_idx], row_mask)
            grad_down = grad_down.at[section_idx, layer_idx].add(owner_sum(select, tile_down))
            grad_up = grad_up.at[section_idx, layer_idx].add(owner_sum(select, up_tiled))
    return (grad_down, grad_up)
```

```python
import jax
import jax.numpy as jnp
from jax import lax
from jax.experimental import pallas as pl
from jax.experimental.pallas import tpu as pltpu
from jax.sharding import PartitionSpec as P

adapter_scale = 0.5
epsilon = 1e-06


def relay_kernel(x_ref, c_ref, slot_ref, down_ref, up_ref, out_ref, hidden_ref, grad_ref):
    sections, rank_columns, width = down_ref.shape
    rows = x_ref.shape[0]
    half = rank_columns // 2
    column_slot = lax.broadcasted_iota(jnp.int32, (rows, rank_columns), 1) // half
    row_mask = slot_ref[...] == column_slot
    hidden_ref[0] = x_ref[...]
    grad_ref[...] = c_ref[...]

    def norm_parts(section):
        hidden = hidden_ref[section].astype(jnp.float32)
        inverse = lax.rsqrt(jnp.mean(hidden * hidden, axis=-1, keepdims=True) + epsilon)
        return hidden, inverse, hidden * inverse

    def forward(section, carried):
        hidden, inverse, unit = norm_parts(section)
        normed = unit.astype(jnp.bfloat16)
        out_ref[section, :, 0:width] = normed
        rank = lax.dot_general(
            normed,
            down_ref[section],
            (((1,), (1,)), ((), ())),
            preferred_element_type=jnp.float32,
        )
        rank = jnp.where(row_mask, rank, 0.0).astype(jnp.bfloat16)
        out_ref[section, :, 2 * width : 2 * width + rank_columns] = rank
        update = jnp.dot(rank, up_ref[section], preferred_element_type=jnp.float32)
        hidden_ref[section + 1] = (hidden + adapter_scale * update).astype(jnp.bfloat16)
        return carried

    lax.fori_loop(0, sections, forward, 0)

    def backward(step, carried):
        section = sections - 1 - step
        hidden, inverse, unit = norm_parts(section)
        grads = grad_ref[...]
        out_ref[section, :, width : 2 * width] = grads
        rank_grads = adapter_scale * lax.dot_general(
            grads,
            up_ref[section],
            (((1,), (1,)), ((), ())),
            preferred_element_type=jnp.float32,
        )
        rank_grads = jnp.where(row_mask, rank_grads, 0.0).astype(jnp.bfloat16)
        out_ref[section, :, 2 * width + 128 : 2 * width + 128 + rank_columns] = rank_grads
        unit_grads = jnp.dot(rank_grads, down_ref[section], preferred_element_type=jnp.float32)
        back = grads.astype(jnp.float32) + inverse * (
            unit_grads - unit * jnp.mean(unit_grads * unit, axis=-1, keepdims=True)
        )
        grad_ref[...] = back.astype(jnp.bfloat16)
        return carried

    lax.fori_loop(0, sections, backward, 0)


def relay(x, c, slot, down_every, up_every):
    sections, rank_columns, width = down_every.shape
    rows = x.shape[0]
    vmem = pl.BlockSpec(memory_space=pltpu.VMEM)
    return pl.pallas_call(
        relay_kernel,
        out_shape=jax.ShapeDtypeStruct((sections, rows, 2 * width + 256), jnp.bfloat16),
        in_specs=[vmem] * 5,
        out_specs=vmem,
        scratch_shapes=[
            pltpu.VMEM((sections + 1, rows, width), jnp.bfloat16),
            pltpu.VMEM((rows, width), jnp.bfloat16),
        ],
        compiler_params=pltpu.CompilerParams(vmem_limit_bytes=48 * 1024 * 1024),
    )(x, c, slot, down_every, up_every)


def body(
    inputs,
    cotangent,
    row_adapter_slot,
    deployed_adapter_ids,
    adapter_owner_device,
    adapter_down_weight,
    adapter_up_weight,
):
    section_index = lax.axis_index("section")
    pieces = lax.axis_size("dp")
    micro_count, row_count, width = inputs.shape
    slot_count = adapter_down_weight.shape[3]
    rank = adapter_down_weight.shape[4]
    rank_columns = slot_count * rank
    down_every = lax.all_gather(adapter_down_weight.reshape(rank_columns, width), "section")
    up_every = lax.all_gather(adapter_up_weight.reshape(rank_columns, width), "section")
    x = lax.dynamic_index_in_dim(inputs, section_index, 0, keepdims=False)
    c = lax.dynamic_index_in_dim(cotangent, section_index, 0, keepdims=False)
    slot = lax.dynamic_index_in_dim(row_adapter_slot, section_index, 0, keepdims=False)
    packed = relay(x, c, slot[:, None], down_every, up_every)
    packed = lax.all_to_all(packed, "section", split_axis=0, concat_axis=0, tiled=True)
    packed = packed.reshape(micro_count * row_count, 2 * width + 256)
    normed = packed[:, :width]
    grads = packed[:, width : 2 * width]
    rank_rows = packed[:, 2 * width : 2 * width + rank_columns]
    rank_grads = packed[:, 2 * width + 128 : 2 * width + 128 + rank_columns]

    def tile(rank_values, row_values):
        return jnp.concatenate(
            [
                lax.dot_general(
                    rank_values[:, k * rank : (k + 1) * rank],
                    row_values,
                    (((0,), (0,)), ((), ())),
                    preferred_element_type=jnp.float32,
                )
                for k in range(slot_count)
            ],
            axis=-1,
        )

    tiles = jnp.concatenate(
        [tile(rank_grads, normed), adapter_scale * tile(rank_rows, grads)], axis=0
    ).astype(jnp.bfloat16)
    lanes = width // 128
    tiles = tiles.reshape(pieces, slot_count * lanes, 128)
    tiles = lax.all_to_all(tiles, "dp", split_axis=0, concat_axis=0, tiled=True)
    tiles = tiles.reshape(pieces, slot_count, width)
    adapter_ids = jnp.arange(adapter_owner_device.shape[0], dtype=jnp.int32)
    owner_of = jnp.sum(
        jnp.where(deployed_adapter_ids[..., None] == adapter_ids, adapter_owner_device, 0), axis=-1
    )
    owner_ids = jnp.arange(pieces, dtype=jnp.int32)
    select = (owner_of[None, :, :] == owner_ids[:, None, None]).astype(jnp.bfloat16)
    owned = jnp.einsum("odk,dkx->ox", select, tiles, preferred_element_type=jnp.float32)
    owned = owned.astype(jnp.bfloat16).reshape(pieces, lanes, 128)
    final = lax.all_to_all(owned, "dp", split_axis=0, concat_axis=0, tiled=True)
    final = final.reshape(2, 1, 1, 1, rank, width).astype(jnp.float32)
    return (final[0], final[1])


def solution(mesh):
    placed = (
        P(None, "dp", None),
        P(None, "dp", None),
        P(None, "dp"),
        P(),
        P(),
        P("section", None, "dp", None, None, None),
        P("section", None, "dp", None, None, None),
    )
    return jax.shard_map(
        body,
        mesh=mesh,
        in_specs=placed,
        out_specs=(P("section", None, "dp", None, None), P("section", None, "dp", None, None)),
        check_vma=False,
    )
```

```python
import jax
import jax.numpy as jnp
from jax import lax
from jax.experimental import pallas as pl
from jax.experimental.pallas import tpu as pltpu
from jax.sharding import PartitionSpec as P

adapter_scale = 0.5
epsilon = 1e-06


MESH = pl.DeviceIdType.MESH


def relay_kernel(
    x_ref,
    c_ref,
    slot_ref,
    down_ref,
    up_ref,
    normed_ref,
    grads_ref,
    weights,
    hidden_ref,
    grad_ref,
    normed_out,
    grads_out,
    own_sem,
    gather_send,
    gather_recv,
    rows_send,
    rows_recv,
):
    sections, unused_pair, rank_columns, width = weights.shape
    rows = x_ref.shape[0]
    half = rank_columns // 2
    me = lax.axis_index("section")
    core = lax.rem(me, 2)
    partner = me + 1 - 2 * core
    right = lax.rem(me + 2, sections)
    left = lax.rem(me + sections - 2, sections)
    far = lax.rem(me + 4, sections)

    barrier = pltpu.get_barrier_semaphore()
    for step in range(1, sections):
        pl.semaphore_signal(
            barrier,
            inc=1,
            device_id={"section": lax.rem(me + step, sections)},
            device_id_type=MESH,
        )
    pl.semaphore_wait(barrier, sections - 1)

    def pass_on(number, src, owner, which, target):
        return pltpu.make_async_remote_copy(
            src_ref=src,
            dst_ref=weights.at[owner, which],
            send_sem=gather_send.at[number],
            recv_sem=gather_recv.at[number],
            device_id={"section": target},
            device_id_type=MESH,
        )

    def forwarded(number, owner, which, target):
        return pass_on(number, weights.at[owner, which], owner, which, target)

    copies = [
        pass_on(0, down_ref, me, 0, right),
        pass_on(1, up_ref, me, 1, left),
        pass_on(2, up_ref, me, 1, right),
        pass_on(3, down_ref, me, 0, left),
        pass_on(4, down_ref, me, 0, partner),
        pass_on(5, up_ref, me, 1, partner),
    ]
    for copy in copies:
        copy.start()
    own = [
        pltpu.make_async_copy(down_ref, weights.at[me, 0], own_sem.at[0]),
        pltpu.make_async_copy(up_ref, weights.at[me, 1], own_sem.at[1]),
    ]
    for copy in own:
        copy.start()

    def send_on(number, owner, which, target):
        copy = forwarded(number, owner, which, target)
        copy.start()
        copies.append(copy)

    copies[0].wait_recv()
    send_on(6, left, 0, right)
    send_on(8, left, 0, partner)
    copies[1].wait_recv()
    send_on(7, right, 1, left)
    send_on(9, right, 1, partner)
    copies[2].wait_recv()
    send_on(10, left, 1, partner)
    copies[3].wait_recv()
    send_on(11, right, 0, partner)
    copies[6].wait_recv()
    send_on(12, far, 0, partner)
    copies[8].wait_recv()
    send_on(13, far, 1, partner)

    column_slot = lax.broadcasted_iota(jnp.int32, (rows, rank_columns), 1) // half
    row_mask = slot_ref[...] == column_slot
    hidden_ref[0] = x_ref[...]
    grad_ref[...] = c_ref[...]
    for copy in own:
        copy.wait()
    for place in (4, 5, 7, 9, 10, 11, 12, 13):
        copies[place].wait_recv()

    def rows_copy(kind, section, place):
        source, target = ((normed_out, normed_ref), (grads_out, grads_ref))[kind]
        return pltpu.make_async_remote_copy(
            src_ref=source.at[section],
            dst_ref=target.at[place],
            send_sem=rows_send.at[kind, section],
            recv_sem=rows_recv.at[kind, place],
            device_id={"section": section},
            device_id_type=MESH,
        )

    def send_rows(kind, section):
        @pl.when(section != me)
        def start():
            rows_copy(kind, section, me).start()

    def norm_parts(section):
        hidden = hidden_ref[section].astype(jnp.float32)
        inverse = lax.rsqrt(jnp.mean(hidden * hidden, axis=-1, keepdims=True) + epsilon)
        return hidden, inverse, hidden * inverse

    def forward(section, carried):
        hidden, inverse, unit = norm_parts(section)
        normed = unit.astype(jnp.bfloat16)
        normed_out[section, :, 0:width] = normed
        rank = lax.dot_general(
            normed,
            weights[section, 0],
            (((1,), (1,)), ((), ())),
            preferred_element_type=jnp.float32,
        )
        rank = jnp.where(row_mask, rank, 0.0).astype(jnp.bfloat16)
        normed_out[section, :, width : width + rank_columns] = rank
        update = jnp.dot(rank, weights[section, 1], preferred_element_type=jnp.float32)
        hidden_ref[section + 1] = (hidden + adapter_scale * update).astype(jnp.bfloat16)

        @pl.when(section > 0)
        def send_last():
            send_rows(0, section - 1)

        return carried

    lax.fori_loop(0, sections, forward, 0)

    def backward(step, carried):
        section = sections - 1 - step
        hidden, inverse, unit = norm_parts(section)
        grads = grad_ref[...]
        grads_out[section, :, 0:width] = grads
        rank_grads = adapter_scale * lax.dot_general(
            grads,
            weights[section, 1],
            (((1,), (1,)), ((), ())),
            preferred_element_type=jnp.float32,
        )
        rank_grads = jnp.where(row_mask, rank_grads, 0.0).astype(jnp.bfloat16)
        grads_out[section, :, width : width + rank_columns] = rank_grads
        unit_grads = jnp.dot(
            rank_grads, weights[section, 0], preferred_element_type=jnp.float32
        )
        back = grads.astype(jnp.float32) + inverse * (
            unit_grads - unit * jnp.mean(unit_grads * unit, axis=-1, keepdims=True)
        )
        grad_ref[...] = back.astype(jnp.bfloat16)

        @pl.when(step == 0)
        def send_top():
            send_rows(0, sections - 1)

        @pl.when(step > 0)
        def send_last():
            send_rows(1, section + 1)

        return carried

    lax.fori_loop(0, sections, backward, 0)
    normed_ref[me] = normed_out[me]
    grads_ref[me] = grads_out[me]
    send_rows(1, 0)
    for copy in copies:
        copy.wait_send()

    def finish(step, carried):
        other = lax.rem(me + step, sections)
        for kind in range(2):
            copy = rows_copy(kind, other, other)
            copy.wait_send()
            copy.wait_recv()
        return carried

    lax.fori_loop(1, sections, finish, 0)


def relay(x, c, slot, down_weight, up_weight):
    sections = lax.axis_size("section")
    rank_columns, width = down_weight.shape
    rows = x.shape[0]
    vmem = pl.BlockSpec(memory_space=pltpu.VMEM)
    records = (sections, rows, width + 128)
    return pl.pallas_call(
        relay_kernel,
        out_shape=[jax.ShapeDtypeStruct(records, jnp.bfloat16)] * 2,
        in_specs=[vmem] * 5,
        out_specs=[vmem] * 2,
        scratch_shapes=[
            pltpu.VMEM((sections, 2, rank_columns, width), jnp.bfloat16),
            pltpu.VMEM((sections + 1, rows, width), jnp.bfloat16),
            pltpu.VMEM((rows, width), jnp.bfloat16),
            pltpu.VMEM(records, jnp.bfloat16),
            pltpu.VMEM(records, jnp.bfloat16),
            pltpu.SemaphoreType.DMA((2,)),
            pltpu.SemaphoreType.DMA((14,)),
            pltpu.SemaphoreType.DMA((14,)),
            pltpu.SemaphoreType.DMA((2, sections)),
            pltpu.SemaphoreType.DMA((2, sections)),
        ],
        compiler_params=pltpu.CompilerParams(
            collective_id=0, has_side_effects=True, vmem_limit_bytes=48 * 1024 * 1024
        ),
    )(x, c, slot, down_weight, up_weight)


def body(
    inputs,
    cotangent,
    row_adapter_slot,
    deployed_adapter_ids,
    adapter_owner_device,
    adapter_down_weight,
    adapter_up_weight,
):
    section_index = lax.axis_index("section")
    pieces = lax.axis_size("dp")
    micro_count, row_count, width = inputs.shape
    slot_count = adapter_down_weight.shape[3]
    rank = adapter_down_weight.shape[4]
    rank_columns = slot_count * rank
    down_weight = adapter_down_weight.reshape(rank_columns, width)
    up_weight = adapter_up_weight.reshape(rank_columns, width)
    x = lax.dynamic_index_in_dim(inputs, section_index, 0, keepdims=False)
    c = lax.dynamic_index_in_dim(cotangent, section_index, 0, keepdims=False)
    slot = lax.dynamic_index_in_dim(row_adapter_slot, section_index, 0, keepdims=False)
    normed, grads = relay(x, c, slot[:, None], down_weight, up_weight)
    normed = normed.reshape(micro_count * row_count, width + 128)
    grads = grads.reshape(micro_count * row_count, width + 128)
    rank_rows = normed[:, width : width + rank_columns]
    rank_grads = grads[:, width : width + rank_columns]
    normed = normed[:, :width]
    grads = grads[:, :width]

    def tile(rank_values, row_values):
        return jnp.concatenate(
            [
                lax.dot_general(
                    rank_values[:, k * rank : (k + 1) * rank],
                    row_values,
                    (((0,), (0,)), ((), ())),
                    preferred_element_type=jnp.float32,
                )
                for k in range(slot_count)
            ],
            axis=-1,
        )

    tiles = jnp.concatenate(
        [tile(rank_grads, normed), adapter_scale * tile(rank_rows, grads)], axis=0
    ).astype(jnp.bfloat16)
    lanes = width // 128
    tiles = tiles.reshape(pieces, slot_count * lanes, 128)
    tiles = lax.all_to_all(tiles, "dp", split_axis=0, concat_axis=0, tiled=True)
    tiles = tiles.reshape(pieces, slot_count, width)
    adapter_ids = jnp.arange(adapter_owner_device.shape[0], dtype=jnp.int32)
    owner_of = jnp.sum(
        jnp.where(deployed_adapter_ids[..., None] == adapter_ids, adapter_owner_device, 0), axis=-1
    )
    owner_ids = jnp.arange(pieces, dtype=jnp.int32)
    select = (owner_of[None, :, :] == owner_ids[:, None, None]).astype(jnp.bfloat16)
    owned = jnp.einsum("odk,dkx->ox", select, tiles, preferred_element_type=jnp.float32)
    owned = owned.astype(jnp.bfloat16).reshape(pieces, lanes, 128)
    final = lax.all_to_all(owned, "dp", split_axis=0, concat_axis=0, tiled=True)
    final = final.reshape(2, 1, 1, 1, rank, width).astype(jnp.float32)
    return (final[0], final[1])


def solution(mesh):
    placed = (
        P(None, "dp", None),
        P(None, "dp", None),
        P(None, "dp"),
        P(),
        P(),
        P("section", None, "dp", None, None, None),
        P("section", None, "dp", None, None, None),
    )
    return jax.shard_map(
        body,
        mesh=mesh,
        in_specs=placed,
        out_specs=(P("section", None, "dp", None, None), P("section", None, "dp", None, None)),
        check_vma=False,
    )
```

```python
import jax
import jax.numpy as jnp
from jax import lax
from jax.experimental import pallas as pl
from jax.experimental.pallas import tpu as pltpu
from jax.sharding import PartitionSpec as P

adapter_scale = 0.5
epsilon = 1e-06


MESH = pl.DeviceIdType.MESH


def relay_kernel(
    x_ref,
    c_ref,
    slot_ref,
    down_ref,
    up_ref,
    normed_ref,
    grads_ref,
    weights,
    hidden_ref,
    grad_ref,
    normed_out,
    grads_out,
    own_sem,
    gather_send,
    gather_recv,
    rows_send,
    rows_recv,
):
    sections, unused_pair, rank_columns, width = weights.shape
    rows = x_ref.shape[0]
    half = rank_columns // 2
    me = lax.axis_index("section")
    core = lax.rem(me, 2)
    partner = me + 1 - 2 * core
    right = lax.rem(me + 2, sections)
    left = lax.rem(me + sections - 2, sections)
    far = lax.rem(me + 4, sections)

    barrier = pltpu.get_barrier_semaphore()
    for step in range(1, sections):
        pl.semaphore_signal(
            barrier,
            inc=1,
            device_id={"section": lax.rem(me + step, sections)},
            device_id_type=MESH,
        )
    pl.semaphore_wait(barrier, sections - 1)

    def pass_on(number, src, owner, which, target):
        return pltpu.make_async_remote_copy(
            src_ref=src,
            dst_ref=weights.at[owner, which],
            send_sem=gather_send.at[number],
            recv_sem=gather_recv.at[number],
            device_id={"section": target},
            device_id_type=MESH,
        )

    def forwarded(number, owner, which, target):
        return pass_on(number, weights.at[owner, which], owner, which, target)

    copies = [
        pass_on(0, down_ref, me, 0, right),
        pass_on(1, up_ref, me, 1, left),
        pass_on(2, up_ref, me, 1, right),
        pass_on(3, down_ref, me, 0, left),
        pass_on(4, down_ref, me, 0, partner),
        pass_on(5, up_ref, me, 1, partner),
    ]
    for copy in copies:
        copy.start()
    own = [
        pltpu.make_async_copy(down_ref, weights.at[me, 0], own_sem.at[0]),
        pltpu.make_async_copy(up_ref, weights.at[me, 1], own_sem.at[1]),
    ]
    for copy in own:
        copy.start()

    def send_on(number, owner, which, target):
        copy = forwarded(number, owner, which, target)
        copy.start()
        copies.append(copy)

    copies[0].wait_recv()
    send_on(6, left, 0, right)
    send_on(8, left, 0, partner)
    copies[1].wait_recv()
    send_on(7, right, 1, left)
    send_on(9, right, 1, partner)
    copies[2].wait_recv()
    send_on(10, left, 1, partner)
    copies[3].wait_recv()
    send_on(11, right, 0, partner)
    copies[6].wait_recv()
    send_on(12, far, 0, partner)
    copies[8].wait_recv()
    send_on(13, far, 1, partner)

    column_slot = lax.broadcasted_iota(jnp.int32, (rows, rank_columns), 1) // half
    row_mask = slot_ref[...] == column_slot
    hidden_ref[0] = x_ref[...]
    grad_ref[...] = c_ref[...]
    for copy in own:
        copy.wait()
    for place in (4, 5, 7, 9, 10, 11, 12, 13):
        copies[place].wait_recv()

    def rows_copy(kind, section, place):
        source, target = ((normed_out, normed_ref), (grads_out, grads_ref))[kind]
        return pltpu.make_async_remote_copy(
            src_ref=source.at[section],
            dst_ref=target.at[place],
            send_sem=rows_send.at[kind, section],
            recv_sem=rows_recv.at[kind, place],
            device_id={"section": section},
            device_id_type=MESH,
        )

    def send_rows(kind, section):
        @pl.when(section != me)
        def start():
            rows_copy(kind, section, me).start()

    def norm_parts(section):
        hidden = hidden_ref[section].astype(jnp.float32)
        inverse = lax.rsqrt(jnp.mean(hidden * hidden, axis=-1, keepdims=True) + epsilon)
        return hidden, inverse, hidden * inverse

    def forward(section, carried):
        hidden, inverse, unit = norm_parts(section)
        normed = unit.astype(jnp.bfloat16)
        normed_out[section, :, 0:width] = normed
        rank = lax.dot_general(
            normed,
            weights[section, 0],
            (((1,), (1,)), ((), ())),
            preferred_element_type=jnp.float32,
        )
        rank = jnp.where(row_mask, rank, 0.0).astype(jnp.bfloat16)
        normed_out[section, :, width : width + rank_columns] = rank
        update = jnp.dot(rank, weights[section, 1], preferred_element_type=jnp.float32)
        hidden_ref[section + 1] = (hidden + adapter_scale * update).astype(jnp.bfloat16)

        @pl.when(section > 0)
        def send_last():
            send_rows(0, section - 1)

        return carried

    lax.fori_loop(0, sections, forward, 0)

    def backward(step, carried):
        section = sections - 1 - step
        hidden, inverse, unit = norm_parts(section)
        grads = grad_ref[...]
        grads_out[section, :, 0:width] = grads
        rank_grads = adapter_scale * lax.dot_general(
            grads,
            weights[section, 1],
            (((1,), (1,)), ((), ())),
            preferred_element_type=jnp.float32,
        )
        rank_grads = jnp.where(row_mask, rank_grads, 0.0).astype(jnp.bfloat16)
        grads_out[section, :, width : width + rank_columns] = rank_grads
        unit_grads = jnp.dot(
            rank_grads, weights[section, 0], preferred_element_type=jnp.float32
        )
        back = grads.astype(jnp.float32) + inverse * (
            unit_grads - unit * jnp.mean(unit_grads * unit, axis=-1, keepdims=True)
        )
        grad_ref[...] = back.astype(jnp.bfloat16)

        @pl.when(step == 0)
        def send_top():
            send_rows(0, sections - 1)

        @pl.when(step > 0)
        def send_last():
            send_rows(1, section + 1)

        return carried

    lax.fori_loop(0, sections, backward, 0)
    normed_ref[me] = normed_out[me]
    grads_ref[me] = grads_out[me]
    send_rows(1, 0)
    for copy in copies:
        copy.wait_send()

    def finish(step, carried):
        other = lax.rem(me + step, sections)
        for kind in range(2):
            copy = rows_copy(kind, other, other)
            copy.wait_send()
            copy.wait_recv()
        return carried

    lax.fori_loop(1, sections, finish, 0)


def relay(x, c, slot, down_weight, up_weight):
    sections = lax.axis_size("section")
    rank_columns, width = down_weight.shape
    rows = x.shape[0]
    vmem = pl.BlockSpec(memory_space=pltpu.VMEM)
    records = (sections, rows, width + 128)
    return pl.pallas_call(
        relay_kernel,
        out_shape=[jax.ShapeDtypeStruct(records, jnp.bfloat16)] * 2,
        in_specs=[vmem] * 5,
        out_specs=[vmem] * 2,
        scratch_shapes=[
            pltpu.VMEM((sections, 2, rank_columns, width), jnp.bfloat16),
            pltpu.VMEM((sections + 1, rows, width), jnp.bfloat16),
            pltpu.VMEM((rows, width), jnp.bfloat16),
            pltpu.VMEM(records, jnp.bfloat16),
            pltpu.VMEM(records, jnp.bfloat16),
            pltpu.SemaphoreType.DMA((2,)),
            pltpu.SemaphoreType.DMA((14,)),
            pltpu.SemaphoreType.DMA((14,)),
            pltpu.SemaphoreType.DMA((2, sections)),
            pltpu.SemaphoreType.DMA((2, sections)),
        ],
        compiler_params=pltpu.CompilerParams(
            collective_id=0, has_side_effects=True, vmem_limit_bytes=48 * 1024 * 1024
        ),
    )(x, c, slot, down_weight, up_weight)


def owners_kernel(
    tiles_ref, select_ref, out_ref, pieces_in, owned, own_sem, send_sem, recv_sem
):
    pieces = tiles_ref.shape[0]
    slot_count = select_ref.shape[0]
    lanes = tiles_ref.shape[1] // slot_count
    side = 8
    me = lax.axis_index("dp")
    me_z, me_y = lax.div(me, side), lax.rem(me, side)

    def peer(step):
        z = lax.rem(me_z + lax.div(step, side), side)
        y = lax.rem(me_y + lax.rem(step, side), side)
        return z * side + y

    barrier = pltpu.get_barrier_semaphore()

    def greet(step, carried):
        pl.semaphore_signal(
            barrier, inc=1, device_id={"dp": peer(step)}, device_id_type=MESH
        )
        return carried

    lax.fori_loop(1, pieces, greet, 0)
    pl.semaphore_wait(barrier, pieces - 1)

    def piece_copy(stage, other, place):
        source, target = ((tiles_ref, pieces_in), (owned, out_ref))[stage]
        return pltpu.make_async_remote_copy(
            src_ref=source.at[other],
            dst_ref=target.at[place],
            send_sem=send_sem.at[stage, other],
            recv_sem=recv_sem.at[stage, place],
            device_id={"dp": other},
            device_id_type=MESH,
        )

    def send(stage):
        def one(step, carried):
            piece_copy(stage, peer(step), me).start()
            return carried

        lax.fori_loop(1, pieces, one, 0)

    def receive(stage):
        def one(step, carried):
            other = peer(step)
            piece_copy(stage, other, other).wait_recv()
            return carried

        lax.fori_loop(1, pieces, one, 0)

    send(0)
    own = pltpu.make_async_copy(tiles_ref.at[me], pieces_in.at[me], own_sem.at[0])
    own.start()
    own.wait()
    receive(0)
    by_lanes = jnp.swapaxes(pieces_in[...], 0, 1)
    sums = []
    for lane in range(lanes):
        total = None
        for k in range(slot_count):
            term = jnp.dot(
                select_ref[k], by_lanes[k * lanes + lane], preferred_element_type=jnp.float32
            )
            total = term if total is None else total + term
        sums.append(total.astype(jnp.bfloat16))
    owned[...] = jnp.swapaxes(jnp.stack(sums), 0, 1)
    send(1)
    out_ref[me] = owned[me]
    receive(1)

    def finish(step, carried):
        other = peer(step)
        for stage in range(2):
            piece_copy(stage, other, other).wait_send()
        return carried

    lax.fori_loop(1, pieces, finish, 0)


def to_owners(tiles, select):
    pieces, blocks, columns = tiles.shape
    lanes = blocks // select.shape[0]
    vmem = pl.BlockSpec(memory_space=pltpu.VMEM)
    return pl.pallas_call(
        owners_kernel,
        out_shape=jax.ShapeDtypeStruct((pieces, lanes, columns), jnp.bfloat16),
        in_specs=[vmem] * 2,
        out_specs=vmem,
        scratch_shapes=[
            pltpu.VMEM((pieces, blocks, columns), jnp.bfloat16),
            pltpu.VMEM((pieces, lanes, columns), jnp.bfloat16),
            pltpu.SemaphoreType.DMA((1,)),
            pltpu.SemaphoreType.DMA((2, pieces)),
            pltpu.SemaphoreType.DMA((2, pieces)),
        ],
        compiler_params=pltpu.CompilerParams(
            collective_id=1, has_side_effects=True, vmem_limit_bytes=32 * 1024 * 1024
        ),
    )(tiles, select)


def body(
    inputs,
    cotangent,
    row_adapter_slot,
    deployed_adapter_ids,
    adapter_owner_device,
    adapter_down_weight,
    adapter_up_weight,
):
    section_index = lax.axis_index("section")
    pieces = lax.axis_size("dp")
    micro_count, row_count, width = inputs.shape
    slot_count = adapter_down_weight.shape[3]
    rank = adapter_down_weight.shape[4]
    rank_columns = slot_count * rank
    down_weight = adapter_down_weight.reshape(rank_columns, width)
    up_weight = adapter_up_weight.reshape(rank_columns, width)
    x = lax.dynamic_index_in_dim(inputs, section_index, 0, keepdims=False)
    c = lax.dynamic_index_in_dim(cotangent, section_index, 0, keepdims=False)
    slot = lax.dynamic_index_in_dim(row_adapter_slot, section_index, 0, keepdims=False)
    normed, grads = relay(x, c, slot[:, None], down_weight, up_weight)
    normed = normed.reshape(micro_count * row_count, width + 128)
    grads = grads.reshape(micro_count * row_count, width + 128)
    rank_rows = normed[:, width : width + rank_columns]
    rank_grads = grads[:, width : width + rank_columns]
    normed = normed[:, :width]
    grads = grads[:, :width]

    def tile(rank_values, row_values):
        return jnp.concatenate(
            [
                lax.dot_general(
                    rank_values[:, k * rank : (k + 1) * rank],
                    row_values,
                    (((0,), (0,)), ((), ())),
                    preferred_element_type=jnp.float32,
                )
                for k in range(slot_count)
            ],
            axis=-1,
        )

    tiles = jnp.concatenate(
        [tile(rank_grads, normed), adapter_scale * tile(rank_rows, grads)], axis=0
    ).astype(jnp.bfloat16)
    lanes = width // 128
    tiles = tiles.reshape(pieces, slot_count * lanes, 128)
    adapter_ids = jnp.arange(adapter_owner_device.shape[0], dtype=jnp.int32)
    owner_of = jnp.sum(
        jnp.where(deployed_adapter_ids[..., None] == adapter_ids, adapter_owner_device, 0), axis=-1
    )
    owner_ids = jnp.arange(pieces, dtype=jnp.int32)
    select = (owner_of.T[:, None, :] == owner_ids[None, :, None]).astype(jnp.bfloat16)
    final = to_owners(tiles, select)
    final = final.reshape(2, 1, 1, 1, rank, width).astype(jnp.float32)
    return (final[0], final[1])


def solution(mesh):
    placed = (
        P(None, "dp", None),
        P(None, "dp", None),
        P(None, "dp"),
        P(),
        P(),
        P("section", None, "dp", None, None, None),
        P("section", None, "dp", None, None, None),
    )
    return jax.shard_map(
        body,
        mesh=mesh,
        in_specs=placed,
        out_specs=(P("section", None, "dp", None, None), P("section", None, "dp", None, None)),
        check_vma=False,
    )
```

```python
import jax
import jax.numpy as jnp
from jax import lax
from jax.experimental import pallas as pl
from jax.experimental.pallas import tpu as pltpu
from jax.sharding import PartitionSpec as P

adapter_scale = 0.5
epsilon = 1e-06


MESH = pl.DeviceIdType.MESH


def relay_kernel(
    x_ref,
    c_ref,
    slot_ref,
    down_ref,
    up_ref,
    normed_ref,
    grads_ref,
    weights,
    hidden_ref,
    grad_ref,
    normed_out,
    grads_out,
    own_sem,
    gather_send,
    gather_recv,
    rows_send,
    rows_recv,
):
    sections, unused_pair, rank_columns, width = weights.shape
    rows = x_ref.shape[0]
    half = rank_columns // 2
    me = lax.axis_index("section")
    core = lax.rem(me, 2)
    partner = me + 1 - 2 * core
    right = lax.rem(me + 2, sections)
    left = lax.rem(me + sections - 2, sections)
    far = lax.rem(me + 4, sections)

    barrier = pltpu.get_barrier_semaphore()
    for step in range(1, sections):
        pl.semaphore_signal(
            barrier,
            inc=1,
            device_id={"section": lax.rem(me + step, sections)},
            device_id_type=MESH,
        )
    pl.semaphore_wait(barrier, sections - 1)

    def pass_on(number, src, owner, which, target):
        return pltpu.make_async_remote_copy(
            src_ref=src,
            dst_ref=weights.at[owner, which],
            send_sem=gather_send.at[number],
            recv_sem=gather_recv.at[number],
            device_id={"section": target},
            device_id_type=MESH,
        )

    def forwarded(number, owner, which, target):
        return pass_on(number, weights.at[owner, which], owner, which, target)

    copies = [
        pass_on(0, down_ref, me, 0, right),
        pass_on(1, up_ref, me, 1, left),
        pass_on(2, up_ref, me, 1, right),
        pass_on(3, down_ref, me, 0, left),
        pass_on(4, down_ref, me, 0, partner),
        pass_on(5, up_ref, me, 1, partner),
    ]
    for copy in copies:
        copy.start()
    own = [
        pltpu.make_async_copy(down_ref, weights.at[me, 0], own_sem.at[0]),
        pltpu.make_async_copy(up_ref, weights.at[me, 1], own_sem.at[1]),
    ]
    for copy in own:
        copy.start()

    def send_on(number, owner, which, target):
        copy = forwarded(number, owner, which, target)
        copy.start()
        copies.append(copy)

    copies[0].wait_recv()
    send_on(6, left, 0, right)
    send_on(8, left, 0, partner)
    copies[1].wait_recv()
    send_on(7, right, 1, left)
    send_on(9, right, 1, partner)
    copies[2].wait_recv()
    send_on(10, left, 1, partner)
    copies[3].wait_recv()
    send_on(11, right, 0, partner)
    copies[6].wait_recv()
    send_on(12, far, 0, partner)
    copies[8].wait_recv()
    send_on(13, far, 1, partner)

    column_slot = lax.broadcasted_iota(jnp.int32, (rows, rank_columns), 1) // half
    row_mask = slot_ref[...] == column_slot
    hidden_ref[0] = x_ref[...]
    grad_ref[...] = c_ref[...]
    for copy in own:
        copy.wait()
    for place in (4, 5, 7, 9, 10, 11, 12, 13):
        copies[place].wait_recv()

    def rows_copy(kind, section, place):
        source, target = ((normed_out, normed_ref), (grads_out, grads_ref))[kind]
        return pltpu.make_async_remote_copy(
            src_ref=source.at[section],
            dst_ref=target.at[place],
            send_sem=rows_send.at[kind, section],
            recv_sem=rows_recv.at[kind, place],
            device_id={"section": section},
            device_id_type=MESH,
        )

    def send_rows(kind, section):
        @pl.when(section != me)
        def start():
            rows_copy(kind, section, me).start()

    def norm_parts(section):
        hidden = hidden_ref[section].astype(jnp.float32)
        inverse = lax.rsqrt(jnp.mean(hidden * hidden, axis=-1, keepdims=True) + epsilon)
        return hidden, inverse, hidden * inverse

    def forward(section, carried):
        hidden, inverse, unit = norm_parts(section)
        normed = unit.astype(jnp.bfloat16)
        normed_out[section, :, 0:width] = normed
        rank = lax.dot_general(
            normed,
            weights[section, 0],
            (((1,), (1,)), ((), ())),
            preferred_element_type=jnp.float32,
        )
        rank = jnp.where(row_mask, rank, 0.0).astype(jnp.bfloat16)
        normed_out[section, :, width : width + rank_columns] = rank
        update = jnp.dot(rank, weights[section, 1], preferred_element_type=jnp.float32)
        hidden_ref[section + 1] = (hidden + adapter_scale * update).astype(jnp.bfloat16)

        @pl.when(section > 0)
        def send_last():
            send_rows(0, section - 1)

        return carried

    lax.fori_loop(0, sections, forward, 0)

    def backward(step, carried):
        section = sections - 1 - step
        hidden, inverse, unit = norm_parts(section)
        grads = grad_ref[...]
        grads_out[section, :, 0:width] = grads
        rank_grads = adapter_scale * lax.dot_general(
            grads,
            weights[section, 1],
            (((1,), (1,)), ((), ())),
            preferred_element_type=jnp.float32,
        )
        rank_grads = jnp.where(row_mask, rank_grads, 0.0).astype(jnp.bfloat16)
        grads_out[section, :, width : width + rank_columns] = rank_grads
        unit_grads = jnp.dot(
            rank_grads, weights[section, 0], preferred_element_type=jnp.float32
        )
        back = grads.astype(jnp.float32) + inverse * (
            unit_grads - unit * jnp.mean(unit_grads * unit, axis=-1, keepdims=True)
        )
        grad_ref[...] = back.astype(jnp.bfloat16)

        @pl.when(step == 0)
        def send_top():
            send_rows(0, sections - 1)

        @pl.when(step > 0)
        def send_last():
            send_rows(1, section + 1)

        return carried

    lax.fori_loop(0, sections, backward, 0)
    normed_ref[me] = normed_out[me]
    grads_ref[me] = grads_out[me]
    send_rows(1, 0)
    for copy in copies:
        copy.wait_send()

    def finish(step, carried):
        other = lax.rem(me + step, sections)
        for kind in range(2):
            copy = rows_copy(kind, other, other)
            copy.wait_send()
            copy.wait_recv()
        return carried

    lax.fori_loop(1, sections, finish, 0)


def relay(x, c, slot, down_weight, up_weight):
    sections = lax.axis_size("section")
    rank_columns, width = down_weight.shape
    rows = x.shape[0]
    vmem = pl.BlockSpec(memory_space=pltpu.VMEM)
    records = (sections, rows, width + 128)
    return pl.pallas_call(
        relay_kernel,
        out_shape=[jax.ShapeDtypeStruct(records, jnp.bfloat16)] * 2,
        in_specs=[vmem] * 5,
        out_specs=[vmem] * 2,
        scratch_shapes=[
            pltpu.VMEM((sections, 2, rank_columns, width), jnp.bfloat16),
            pltpu.VMEM((sections + 1, rows, width), jnp.bfloat16),
            pltpu.VMEM((rows, width), jnp.bfloat16),
            pltpu.VMEM(records, jnp.bfloat16),
            pltpu.VMEM(records, jnp.bfloat16),
            pltpu.SemaphoreType.DMA((2,)),
            pltpu.SemaphoreType.DMA((14,)),
            pltpu.SemaphoreType.DMA((14,)),
            pltpu.SemaphoreType.DMA((2, sections)),
            pltpu.SemaphoreType.DMA((2, sections)),
        ],
        compiler_params=pltpu.CompilerParams(
            collective_id=0, has_side_effects=True, vmem_limit_bytes=48 * 1024 * 1024
        ),
    )(x, c, slot, down_weight, up_weight)


def owners_kernel(
    tiles_ref, select_ref, out_ref, pieces_in, owned, own_sem, send_sem, recv_sem
):
    pieces = tiles_ref.shape[0]
    slot_count = select_ref.shape[0]
    lanes = tiles_ref.shape[1] // slot_count
    side = 8
    me = lax.axis_index("dp")
    me_z, me_y = lax.div(me, side), lax.rem(me, side)

    turn = 1 - 2 * lax.rem(lax.axis_index("section"), 2)

    def peer(step):
        offset = lax.rem(step * 29, pieces)
        z = lax.rem(me_z + turn * lax.div(offset, side) + side, side)
        y = lax.rem(me_y + turn * lax.rem(offset, side) + side, side)
        return z * side + y

    barrier = pltpu.get_barrier_semaphore()

    def greet(step, carried):
        pl.semaphore_signal(
            barrier, inc=1, device_id={"dp": peer(step)}, device_id_type=MESH
        )
        return carried

    lax.fori_loop(1, pieces, greet, 0)
    pl.semaphore_wait(barrier, pieces - 1)

    def piece_copy(stage, other, place):
        source, target = ((tiles_ref, pieces_in), (owned, out_ref))[stage]
        return pltpu.make_async_remote_copy(
            src_ref=source.at[other],
            dst_ref=target.at[place],
            send_sem=send_sem.at[stage, other],
            recv_sem=recv_sem.at[stage, place],
            device_id={"dp": other},
            device_id_type=MESH,
        )

    def send(stage):
        def one(step, carried):
            piece_copy(stage, peer(step), me).start()
            return carried

        lax.fori_loop(1, pieces, one, 0)

    def receive(stage):
        def one(step, carried):
            other = peer(step)
            piece_copy(stage, other, other).wait_recv()
            return carried

        lax.fori_loop(1, pieces, one, 0)

    send(0)
    own = pltpu.make_async_copy(tiles_ref.at[me], pieces_in.at[me], own_sem.at[0])
    own.start()
    own.wait()
    receive(0)
    by_lanes = jnp.swapaxes(pieces_in[...], 0, 1)
    sums = []
    for lane in range(lanes):
        total = None
        for k in range(slot_count):
            term = jnp.dot(
                select_ref[k], by_lanes[k * lanes + lane], preferred_element_type=jnp.float32
            )
            total = term if total is None else total + term
        sums.append(total.astype(jnp.bfloat16))
    owned[...] = jnp.swapaxes(jnp.stack(sums), 0, 1)
    send(1)
    out_ref[me] = owned[me]
    receive(1)

    def finish(step, carried):
        other = peer(step)
        for stage in range(2):
            piece_copy(stage, other, other).wait_send()
        return carried

    lax.fori_loop(1, pieces, finish, 0)


def to_owners(tiles, select):
    pieces, blocks, columns = tiles.shape
    lanes = blocks // select.shape[0]
    vmem = pl.BlockSpec(memory_space=pltpu.VMEM)
    return pl.pallas_call(
        owners_kernel,
        out_shape=jax.ShapeDtypeStruct((pieces, lanes, columns), jnp.bfloat16),
        in_specs=[vmem] * 2,
        out_specs=vmem,
        scratch_shapes=[
            pltpu.VMEM((pieces, blocks, columns), jnp.bfloat16),
            pltpu.VMEM((pieces, lanes, columns), jnp.bfloat16),
            pltpu.SemaphoreType.DMA((1,)),
            pltpu.SemaphoreType.DMA((2, pieces)),
            pltpu.SemaphoreType.DMA((2, pieces)),
        ],
        compiler_params=pltpu.CompilerParams(
            collective_id=1, has_side_effects=True, vmem_limit_bytes=32 * 1024 * 1024
        ),
    )(tiles, select)


def body(
    inputs,
    cotangent,
    row_adapter_slot,
    deployed_adapter_ids,
    adapter_owner_device,
    adapter_down_weight,
    adapter_up_weight,
):
    section_index = lax.axis_index("section")
    pieces = lax.axis_size("dp")
    micro_count, row_count, width = inputs.shape
    slot_count = adapter_down_weight.shape[3]
    rank = adapter_down_weight.shape[4]
    rank_columns = slot_count * rank
    down_weight = adapter_down_weight.reshape(rank_columns, width)
    up_weight = adapter_up_weight.reshape(rank_columns, width)
    x = lax.dynamic_index_in_dim(inputs, section_index, 0, keepdims=False)
    c = lax.dynamic_index_in_dim(cotangent, section_index, 0, keepdims=False)
    slot = lax.dynamic_index_in_dim(row_adapter_slot, section_index, 0, keepdims=False)
    normed, grads = relay(x, c, slot[:, None], down_weight, up_weight)
    normed = normed.reshape(micro_count * row_count, width + 128)
    grads = grads.reshape(micro_count * row_count, width + 128)
    rank_rows = normed[:, width : width + rank_columns]
    rank_grads = grads[:, width : width + rank_columns]
    normed = normed[:, :width]
    grads = grads[:, :width]

    def tile(rank_values, row_values):
        return jnp.concatenate(
            [
                lax.dot_general(
                    rank_values[:, k * rank : (k + 1) * rank],
                    row_values,
                    (((0,), (0,)), ((), ())),
                    preferred_element_type=jnp.float32,
                )
                for k in range(slot_count)
            ],
            axis=-1,
        )

    tiles = jnp.concatenate(
        [tile(rank_grads, normed), adapter_scale * tile(rank_rows, grads)], axis=0
    ).astype(jnp.bfloat16)
    lanes = width // 128
    tiles = tiles.reshape(pieces, slot_count * lanes, 128)
    adapter_ids = jnp.arange(adapter_owner_device.shape[0], dtype=jnp.int32)
    owner_of = jnp.sum(
        jnp.where(deployed_adapter_ids[..., None] == adapter_ids, adapter_owner_device, 0), axis=-1
    )
    owner_ids = jnp.arange(pieces, dtype=jnp.int32)
    select = (owner_of.T[:, None, :] == owner_ids[None, :, None]).astype(jnp.bfloat16)
    final = to_owners(tiles, select)
    final = final.reshape(2, 1, 1, 1, rank, width).astype(jnp.float32)
    return (final[0], final[1])


def solution(mesh):
    placed = (
        P(None, "dp", None),
        P(None, "dp", None),
        P(None, "dp"),
        P(),
        P(),
        P("section", None, "dp", None, None, None),
        P("section", None, "dp", None, None, None),
    )
    return jax.shard_map(
        body,
        mesh=mesh,
        in_specs=placed,
        out_specs=(P("section", None, "dp", None, None), P("section", None, "dp", None, None)),
        check_vma=False,
    )
```

```python
import jax
import jax.numpy as jnp
from jax import lax
from jax.experimental import pallas as pl
from jax.experimental.pallas import tpu as pltpu
from jax.sharding import PartitionSpec as P

adapter_scale = 0.5
epsilon = 1e-06


MESH = pl.DeviceIdType.MESH


def relay_kernel(
    inputs_ref,
    cotangent_ref,
    slot_ref,
    down_ref,
    up_ref,
    select_ref,
    out_ref,
    normed_ref,
    grads_ref,
    weights,
    hidden_ref,
    grad_ref,
    normed_out,
    grads_out,
    own_sem,
    gather_send,
    gather_recv,
    rows_send,
    rows_recv,
    tiles_ref,
    pieces_in,
    owned,
    send_sem,
    recv_sem,
):
    sections, unused_pair, rank_columns, width = weights.shape
    rows = inputs_ref.shape[1]
    half = rank_columns // 2
    me = lax.axis_index("section")
    core = lax.rem(me, 2)
    partner = me + 1 - 2 * core
    right = lax.rem(me + 2, sections)
    left = lax.rem(me + sections - 2, sections)
    far = lax.rem(me + 4, sections)

    pieces = lax.axis_size("dp")
    slot_count = select_ref.shape[0]
    lanes = width // 128
    side = 8
    me_dp = lax.axis_index("dp")
    me_z, me_y = lax.div(me_dp, side), lax.rem(me_dp, side)

    turn = 1 - 2 * core

    def peer(step):
        offset = lax.rem(step * 29, pieces)
        z = lax.rem(me_z + turn * lax.div(offset, side) + side, side)
        y = lax.rem(me_y + turn * lax.rem(offset, side) + side, side)
        return z * side + y

    barrier = pltpu.get_barrier_semaphore()
    for step in range(1, sections):
        pl.semaphore_signal(
            barrier,
            inc=1,
            device_id={"section": lax.rem(me + step, sections)},
            device_id_type=MESH,
        )

    def greet(step, carried):
        pl.semaphore_signal(
            barrier, inc=1, device_id={"dp": peer(step)}, device_id_type=MESH
        )
        return carried

    lax.fori_loop(1, pieces, greet, 0)
    pl.semaphore_wait(barrier, sections - 1 + pieces - 1)

    def pass_on(number, src, owner, which, target):
        return pltpu.make_async_remote_copy(
            src_ref=src,
            dst_ref=weights.at[owner, which],
            send_sem=gather_send.at[number],
            recv_sem=gather_recv.at[number],
            device_id={"section": target},
            device_id_type=MESH,
        )

    def forwarded(number, owner, which, target):
        return pass_on(number, weights.at[owner, which], owner, which, target)

    copies = [
        pass_on(0, down_ref, me, 0, right),
        pass_on(1, up_ref, me, 1, left),
        pass_on(2, up_ref, me, 1, right),
        pass_on(3, down_ref, me, 0, left),
        pass_on(4, down_ref, me, 0, partner),
        pass_on(5, up_ref, me, 1, partner),
    ]
    for copy in copies:
        copy.start()
    own = [
        pltpu.make_async_copy(down_ref, weights.at[me, 0], own_sem.at[0]),
        pltpu.make_async_copy(up_ref, weights.at[me, 1], own_sem.at[1]),
        pltpu.make_async_copy(inputs_ref.at[me], hidden_ref.at[0], own_sem.at[2]),
        pltpu.make_async_copy(cotangent_ref.at[me], grad_ref, own_sem.at[3]),
    ]
    for copy in own:
        copy.start()

    def send_on(number, owner, which, target):
        copy = forwarded(number, owner, which, target)
        copy.start()
        copies.append(copy)

    copies[0].wait_recv()
    send_on(6, left, 0, right)
    send_on(8, left, 0, partner)
    copies[1].wait_recv()
    send_on(7, right, 1, left)
    send_on(9, right, 1, partner)
    copies[2].wait_recv()
    send_on(10, left, 1, partner)
    copies[3].wait_recv()
    send_on(11, right, 0, partner)
    copies[6].wait_recv()
    send_on(12, far, 0, partner)
    copies[8].wait_recv()
    send_on(13, far, 1, partner)

    column_slot = lax.broadcasted_iota(jnp.int32, (rows, rank_columns), 1) // half
    row_mask = slot_ref[...] == column_slot
    for copy in own:
        copy.wait()
    for place in (4, 5, 7, 9, 10, 11, 12, 13):
        copies[place].wait_recv()

    def rows_copy(kind, section, place):
        source, target = ((normed_out, normed_ref), (grads_out, grads_ref))[kind]
        return pltpu.make_async_remote_copy(
            src_ref=source.at[section],
            dst_ref=target.at[place],
            send_sem=rows_send.at[kind, section],
            recv_sem=rows_recv.at[kind, place],
            device_id={"section": section},
            device_id_type=MESH,
        )

    def send_rows(kind, section):
        @pl.when(section != me)
        def start():
            rows_copy(kind, section, me).start()

    def norm_parts(section):
        hidden = hidden_ref[section].astype(jnp.float32)
        inverse = lax.rsqrt(jnp.mean(hidden * hidden, axis=-1, keepdims=True) + epsilon)
        return hidden, inverse, hidden * inverse

    def forward(section, carried):
        hidden, inverse, unit = norm_parts(section)
        normed = unit.astype(jnp.bfloat16)
        normed_out[section, :, 0:width] = normed
        rank = lax.dot_general(
            normed,
            weights[section, 0],
            (((1,), (1,)), ((), ())),
            preferred_element_type=jnp.float32,
        )
        rank = jnp.where(row_mask, rank, 0.0).astype(jnp.bfloat16)
        normed_out[section, :, width : width + rank_columns] = rank
        update = jnp.dot(rank, weights[section, 1], preferred_element_type=jnp.float32)
        hidden_ref[section + 1] = (hidden + adapter_scale * update).astype(jnp.bfloat16)

        @pl.when(section > 0)
        def send_last():
            send_rows(0, section - 1)

        return carried

    lax.fori_loop(0, sections, forward, 0)

    def backward(step, carried):
        section = sections - 1 - step
        hidden, inverse, unit = norm_parts(section)
        grads = grad_ref[...]
        grads_out[section, :, 0:width] = grads
        rank_grads = adapter_scale * lax.dot_general(
            grads,
            weights[section, 1],
            (((1,), (1,)), ((), ())),
            preferred_element_type=jnp.float32,
        )
        rank_grads = jnp.where(row_mask, rank_grads, 0.0).astype(jnp.bfloat16)
        grads_out[section, :, width : width + rank_columns] = rank_grads
        unit_grads = jnp.dot(
            rank_grads, weights[section, 0], preferred_element_type=jnp.float32
        )
        back = grads.astype(jnp.float32) + inverse * (
            unit_grads - unit * jnp.mean(unit_grads * unit, axis=-1, keepdims=True)
        )
        grad_ref[...] = back.astype(jnp.bfloat16)

        @pl.when(step == 0)
        def send_top():
            send_rows(0, sections - 1)

        @pl.when(step > 0)
        def send_last():
            send_rows(1, section + 1)

        return carried

    lax.fori_loop(0, sections, backward, 0)
    normed_ref[me] = normed_out[me]
    grads_ref[me] = grads_out[me]
    send_rows(1, 0)
    for copy in copies:
        copy.wait_send()

    def finish(step, carried):
        other = lax.rem(me + step, sections)
        for kind in range(2):
            copy = rows_copy(kind, other, other)
            copy.wait_send()
            copy.wait_recv()
        return carried

    lax.fori_loop(1, sections, finish, 0)

    tiles = []
    for rank_from, rows_from in ((grads_ref, normed_ref), (normed_ref, grads_ref)):
        rank_values = rank_from[:, :, width : width + rank_columns].reshape(-1, rank_columns)
        row_values = rows_from[:, :, 0:width].reshape(-1, width)
        tile = lax.dot_general(
            rank_values,
            row_values,
            (((0,), (0,)), ((), ())),
            preferred_element_type=jnp.float32,
        )
        if rank_from is normed_ref:
            tile = adapter_scale * tile
        tile = tile.astype(jnp.bfloat16)
        blocks = [
            tile[k * half : (k + 1) * half, 128 * lane : 128 * (lane + 1)]
            for k in range(slot_count)
            for lane in range(lanes)
        ]
        tiles.append(jnp.swapaxes(jnp.stack(blocks), 0, 1))
    tiles_ref[0:half] = tiles[0]
    tiles_ref[half : 2 * half] = tiles[1]

    def piece_copy(stage, other, place):
        source, target = ((tiles_ref, pieces_in), (owned, out_ref))[stage]
        return pltpu.make_async_remote_copy(
            src_ref=source.at[other],
            dst_ref=target.at[place],
            send_sem=send_sem.at[stage, other],
            recv_sem=recv_sem.at[stage, place],
            device_id={"dp": other},
            device_id_type=MESH,
        )

    def send(stage):
        def one(step, carried):
            piece_copy(stage, peer(step), me_dp).start()
            return carried

        lax.fori_loop(1, pieces, one, 0)

    def receive(stage):
        def one(step, carried):
            other = peer(step)
            piece_copy(stage, other, other).wait_recv()
            return carried

        lax.fori_loop(1, pieces, one, 0)

    send(0)
    pieces_in[me_dp] = tiles_ref[me_dp]
    receive(0)
    by_lanes = jnp.swapaxes(pieces_in[...], 0, 1)
    sums = []
    for lane in range(lanes):
        total = None
        for k in range(slot_count):
            term = jnp.dot(
                select_ref[k], by_lanes[k * lanes + lane], preferred_element_type=jnp.float32
            )
            total = term if total is None else total + term
        sums.append(total.astype(jnp.bfloat16))
    owned[...] = jnp.swapaxes(jnp.stack(sums), 0, 1)
    send(1)
    out_ref[me_dp] = owned[me_dp]
    receive(1)

    def drain(step, carried):
        other = peer(step)
        for stage in range(2):
            piece_copy(stage, other, other).wait_send()
        return carried

    lax.fori_loop(1, pieces, drain, 0)


def relay(inputs, cotangent, slot, down_weight, up_weight, select):
    sections = lax.axis_size("section")
    pieces = lax.axis_size("dp")
    rank_columns, width = down_weight.shape
    rows = inputs.shape[1]
    slot_count = select.shape[0]
    lanes = width // 128
    vmem = pl.BlockSpec(memory_space=pltpu.VMEM)
    anywhere = pl.BlockSpec(memory_space=pl.ANY)
    records = (sections, rows, width + 128)
    return pl.pallas_call(
        relay_kernel,
        out_shape=jax.ShapeDtypeStruct((pieces, lanes, 128), jnp.bfloat16),
        in_specs=[anywhere, anywhere, vmem, anywhere, anywhere, vmem],
        out_specs=vmem,
        scratch_shapes=[
            pltpu.VMEM(records, jnp.bfloat16),
            pltpu.VMEM(records, jnp.bfloat16),
            pltpu.VMEM((sections, 2, rank_columns, width), jnp.bfloat16),
            pltpu.VMEM((sections + 1, rows, width), jnp.bfloat16),
            pltpu.VMEM((rows, width), jnp.bfloat16),
            pltpu.VMEM(records, jnp.bfloat16),
            pltpu.VMEM(records, jnp.bfloat16),
            pltpu.SemaphoreType.DMA((4,)),
            pltpu.SemaphoreType.DMA((14,)),
            pltpu.SemaphoreType.DMA((14,)),
            pltpu.SemaphoreType.DMA((2, sections)),
            pltpu.SemaphoreType.DMA((2, sections)),
            pltpu.VMEM((pieces, slot_count * lanes, 128), jnp.bfloat16),
            pltpu.VMEM((pieces, slot_count * lanes, 128), jnp.bfloat16),
            pltpu.VMEM((pieces, lanes, 128), jnp.bfloat16),
            pltpu.SemaphoreType.DMA((2, pieces)),
            pltpu.SemaphoreType.DMA((2, pieces)),
        ],
        compiler_params=pltpu.CompilerParams(
            collective_id=0, has_side_effects=True, vmem_limit_bytes=56 * 1024 * 1024
        ),
    )(inputs, cotangent, slot, down_weight, up_weight, select)


def body(
    inputs,
    cotangent,
    row_adapter_slot,
    deployed_adapter_ids,
    adapter_owner_device,
    adapter_down_weight,
    adapter_up_weight,
):
    section_index = lax.axis_index("section")
    pieces = lax.axis_size("dp")
    micro_count, row_count, width = inputs.shape
    slot_count = adapter_down_weight.shape[3]
    rank = adapter_down_weight.shape[4]
    rank_columns = slot_count * rank
    down_weight = adapter_down_weight.reshape(rank_columns, width)
    up_weight = adapter_up_weight.reshape(rank_columns, width)
    slot = lax.dynamic_index_in_dim(row_adapter_slot, section_index, 0, keepdims=False)
    adapter_ids = jnp.arange(adapter_owner_device.shape[0], dtype=jnp.int32)
    owner_of = jnp.sum(
        jnp.where(deployed_adapter_ids[..., None] == adapter_ids, adapter_owner_device, 0), axis=-1
    )
    owner_ids = jnp.arange(pieces, dtype=jnp.int32)
    select = (owner_of.T[:, None, :] == owner_ids[None, :, None]).astype(jnp.bfloat16)
    final = relay(inputs, cotangent, slot[:, None], down_weight, up_weight, select)
    final = final.reshape(2, 1, 1, 1, rank, width).astype(jnp.float32)
    return (final[0], final[1])


def solution(mesh):
    placed = (
        P(None, "dp", None),
        P(None, "dp", None),
        P(None, "dp"),
        P(),
        P(),
        P("section", None, "dp", None, None, None),
        P("section", None, "dp", None, None, None),
    )
    return jax.shard_map(
        body,
        mesh=mesh,
        in_specs=placed,
        out_specs=(P("section", None, "dp", None, None), P("section", None, "dp", None, None)),
        check_vma=False,
    )
```

```python
import jax
import jax.numpy as jnp
from jax import lax
from jax.experimental import pallas as pl
from jax.experimental.pallas import tpu as pltpu
from jax.sharding import PartitionSpec as P

adapter_scale = 0.5
epsilon = 1e-06


MESH = pl.DeviceIdType.MESH


def relay_kernel(
    inputs_ref,
    cotangent_ref,
    slot_ref,
    down_ref,
    up_ref,
    select_ref,
    out_ref,
    normed_ref,
    grads_ref,
    weights,
    hidden_ref,
    grad_ref,
    normed_out,
    grads_out,
    own_sem,
    gather_send,
    gather_recv,
    rows_send,
    rows_recv,
    tiles_ref,
    pieces_in,
    owned,
    send_sem,
    recv_sem,
    relayed,
    relay_send,
    relay_recv,
):
    sections, unused_pair, rank_columns, width = weights.shape
    rows = inputs_ref.shape[1]
    half = rank_columns // 2
    me = lax.axis_index("section")
    core = lax.rem(me, 2)
    partner = me + 1 - 2 * core
    right = lax.rem(me + 2, sections)
    left = lax.rem(me + sections - 2, sections)
    far = lax.rem(me + 4, sections)

    pieces = lax.axis_size("dp")
    slot_count = select_ref.shape[0]
    lanes = width // 128
    side = 8
    me_dp = lax.axis_index("dp")
    me_z, me_y = lax.div(me_dp, side), lax.rem(me_dp, side)

    turn = 1 - 2 * core

    def peer(step):
        offset = lax.rem(step * 29, pieces)
        z = lax.rem(me_z + turn * lax.div(offset, side) + side, side)
        y = lax.rem(me_y + turn * lax.rem(offset, side) + side, side)
        return z * side + y

    barrier = pltpu.get_barrier_semaphore()
    for step in range(1, sections):
        pl.semaphore_signal(
            barrier,
            inc=1,
            device_id={"section": lax.rem(me + step, sections)},
            device_id_type=MESH,
        )

    def greet(step, carried):
        pl.semaphore_signal(
            barrier, inc=1, device_id={"dp": peer(step)}, device_id_type=MESH
        )
        return carried

    lax.fori_loop(1, pieces, greet, 0)
    pl.semaphore_wait(barrier, sections - 1 + pieces - 1)

    def pass_on(number, src, owner, which, target):
        return pltpu.make_async_remote_copy(
            src_ref=src,
            dst_ref=weights.at[owner, which],
            send_sem=gather_send.at[number],
            recv_sem=gather_recv.at[number],
            device_id={"section": target},
            device_id_type=MESH,
        )

    def forwarded(number, owner, which, target):
        return pass_on(number, weights.at[owner, which], owner, which, target)

    copies = [
        pass_on(0, down_ref, me, 0, right),
        pass_on(1, up_ref, me, 1, left),
        pass_on(2, up_ref, me, 1, right),
        pass_on(3, down_ref, me, 0, left),
        pass_on(4, down_ref, me, 0, partner),
        pass_on(5, up_ref, me, 1, partner),
    ]
    for copy in copies:
        copy.start()
    own = [
        pltpu.make_async_copy(down_ref, weights.at[me, 0], own_sem.at[0]),
        pltpu.make_async_copy(up_ref, weights.at[me, 1], own_sem.at[1]),
        pltpu.make_async_copy(inputs_ref.at[me], hidden_ref.at[0], own_sem.at[2]),
        pltpu.make_async_copy(cotangent_ref.at[me], grad_ref, own_sem.at[3]),
    ]
    for copy in own:
        copy.start()

    def send_on(number, owner, which, target):
        copy = forwarded(number, owner, which, target)
        copy.start()
        copies.append(copy)

    copies[0].wait_recv()
    send_on(6, left, 0, right)
    send_on(8, left, 0, partner)
    copies[1].wait_recv()
    send_on(7, right, 1, left)
    send_on(9, right, 1, partner)
    copies[2].wait_recv()
    send_on(10, left, 1, partner)
    copies[3].wait_recv()
    send_on(11, right, 0, partner)
    copies[6].wait_recv()
    send_on(12, far, 0, partner)
    copies[8].wait_recv()
    send_on(13, far, 1, partner)

    column_slot = lax.broadcasted_iota(jnp.int32, (rows, rank_columns), 1) // half
    row_mask = slot_ref[...] == column_slot
    for copy in own:
        copy.wait()
    for place in (4, 5, 7, 9, 10, 11, 12, 13):
        copies[place].wait_recv()

    def rows_copy(kind, section, place):
        source, target = ((normed_out, normed_ref), (grads_out, grads_ref))[kind]
        return pltpu.make_async_remote_copy(
            src_ref=source.at[section],
            dst_ref=target.at[place],
            send_sem=rows_send.at[kind, section],
            recv_sem=rows_recv.at[kind, place],
            device_id={"section": section},
            device_id_type=MESH,
        )

    def to_left(section):
        which = lax.rem(section, 2)
        return pltpu.make_async_remote_copy(
            src_ref=normed_out.at[section],
            dst_ref=relayed.at[which],
            send_sem=rows_send.at[0, section],
            recv_sem=relay_recv.at[which],
            device_id={"section": left},
            device_id_type=MESH,
        )

    def from_right(which):
        return pltpu.make_async_remote_copy(
            src_ref=relayed.at[which],
            dst_ref=normed_ref.at[right],
            send_sem=relay_send.at[which],
            recv_sem=rows_recv.at[0, right],
            device_id={"section": left - core + which},
            device_id_type=MESH,
        )

    def send_rows(kind, section):
        if kind == 1:

            @pl.when(section != me)
            def start():
                rows_copy(kind, section, me).start()

            return
        opposite = lax.div(section, 2) == lax.div(far, 2)

        @pl.when(opposite)
        def start_left():
            to_left(section).start()

        @pl.when(jnp.logical_not(opposite) & (section != me))
        def start_direct():
            rows_copy(kind, section, me).start()

    def norm_parts(section):
        hidden = hidden_ref[section].astype(jnp.float32)
        inverse = lax.rsqrt(jnp.mean(hidden * hidden, axis=-1, keepdims=True) + epsilon)
        return hidden, inverse, hidden * inverse

    def forward(section, carried):
        hidden, inverse, unit = norm_parts(section)
        normed = unit.astype(jnp.bfloat16)
        normed_out[section, :, 0:width] = normed
        rank = lax.dot_general(
            normed,
            weights[section, 0],
            (((1,), (1,)), ((), ())),
            preferred_element_type=jnp.float32,
        )
        rank = jnp.where(row_mask, rank, 0.0).astype(jnp.bfloat16)
        normed_out[section, :, width : width + rank_columns] = rank
        update = jnp.dot(rank, weights[section, 1], preferred_element_type=jnp.float32)
        hidden_ref[section + 1] = (hidden + adapter_scale * update).astype(jnp.bfloat16)

        @pl.when(section > 0)
        def send_last():
            send_rows(0, section - 1)

        return carried

    lax.fori_loop(0, sections, forward, 0)

    def backward(step, carried):
        section = sections - 1 - step
        hidden, inverse, unit = norm_parts(section)
        grads = grad_ref[...]
        grads_out[section, :, 0:width] = grads
        rank_grads = adapter_scale * lax.dot_general(
            grads,
            weights[section, 1],
            (((1,), (1,)), ((), ())),
            preferred_element_type=jnp.float32,
        )
        rank_grads = jnp.where(row_mask, rank_grads, 0.0).astype(jnp.bfloat16)
        grads_out[section, :, width : width + rank_columns] = rank_grads
        unit_grads = jnp.dot(
            rank_grads, weights[section, 0], preferred_element_type=jnp.float32
        )
        back = grads.astype(jnp.float32) + inverse * (
            unit_grads - unit * jnp.mean(unit_grads * unit, axis=-1, keepdims=True)
        )
        grad_ref[...] = back.astype(jnp.bfloat16)

        @pl.when(step == 0)
        def send_top():
            send_rows(0, sections - 1)

        @pl.when(step > 0)
        def send_last():
            send_rows(1, section + 1)

        @pl.when(step == 5)
        def send_relayed():
            for which in range(2):
                to_left(which).wait_recv()
                from_right(which).start()

        return carried

    lax.fori_loop(0, sections, backward, 0)
    normed_ref[me] = normed_out[me]
    grads_ref[me] = grads_out[me]
    send_rows(1, 0)
    for copy in copies:
        copy.wait_send()

    def finish(step, carried):
        other = lax.rem(me + step, sections)
        for kind in range(2):
            copy = rows_copy(kind, other, other)
            copy.wait_send()
            copy.wait_recv()
        return carried

    lax.fori_loop(1, sections, finish, 0)
    for which in range(2):
        from_right(which).wait_send()

    tiles = []
    for rank_from, rows_from in ((grads_ref, normed_ref), (normed_ref, grads_ref)):
        rank_values = rank_from[:, :, width : width + rank_columns].reshape(-1, rank_columns)
        row_values = rows_from[:, :, 0:width].reshape(-1, width)
        tile = lax.dot_general(
            rank_values,
            row_values,
            (((0,), (0,)), ((), ())),
            preferred_element_type=jnp.float32,
        )
        if rank_from is normed_ref:
            tile = adapter_scale * tile
        tile = tile.astype(jnp.bfloat16)
        blocks = [
            tile[k * half : (k + 1) * half, 128 * lane : 128 * (lane + 1)]
            for k in range(slot_count)
            for lane in range(lanes)
        ]
        tiles.append(jnp.swapaxes(jnp.stack(blocks), 0, 1))
    tiles_ref[0:half] = tiles[0]
    tiles_ref[half : 2 * half] = tiles[1]

    def piece_copy(stage, other, place):
        source, target = ((tiles_ref, pieces_in), (owned, out_ref))[stage]
        return pltpu.make_async_remote_copy(
            src_ref=source.at[other],
            dst_ref=target.at[place],
            send_sem=send_sem.at[stage, other],
            recv_sem=recv_sem.at[stage, place],
            device_id={"dp": other},
            device_id_type=MESH,
        )

    def send(stage):
        def one(step, carried):
            piece_copy(stage, peer(step), me_dp).start()
            return carried

        lax.fori_loop(1, pieces, one, 0)

    def receive(stage):
        def one(step, carried):
            other = peer(step)
            piece_copy(stage, other, other).wait_recv()
            return carried

        lax.fori_loop(1, pieces, one, 0)

    send(0)
    pieces_in[me_dp] = tiles_ref[me_dp]
    receive(0)
    by_lanes = jnp.swapaxes(pieces_in[...], 0, 1)
    sums = []
    for lane in range(lanes):
        total = None
        for k in range(slot_count):
            term = jnp.dot(
                select_ref[k], by_lanes[k * lanes + lane], preferred_element_type=jnp.float32
            )
            total = term if total is None else total + term
        sums.append(total.astype(jnp.bfloat16))
    owned[...] = jnp.swapaxes(jnp.stack(sums), 0, 1)
    send(1)
    out_ref[me_dp] = owned[me_dp]
    receive(1)

    def drain(step, carried):
        other = peer(step)
        for stage in range(2):
            piece_copy(stage, other, other).wait_send()
        return carried

    lax.fori_loop(1, pieces, drain, 0)


def relay(inputs, cotangent, slot, down_weight, up_weight, select):
    sections = lax.axis_size("section")
    pieces = lax.axis_size("dp")
    rank_columns, width = down_weight.shape
    rows = inputs.shape[1]
    slot_count = select.shape[0]
    lanes = width // 128
    vmem = pl.BlockSpec(memory_space=pltpu.VMEM)
    anywhere = pl.BlockSpec(memory_space=pl.ANY)
    records = (sections, rows, width + 128)
    return pl.pallas_call(
        relay_kernel,
        out_shape=jax.ShapeDtypeStruct((pieces, lanes, 128), jnp.bfloat16),
        in_specs=[anywhere, anywhere, vmem, anywhere, anywhere, vmem],
        out_specs=vmem,
        scratch_shapes=[
            pltpu.VMEM(records, jnp.bfloat16),
            pltpu.VMEM(records, jnp.bfloat16),
            pltpu.VMEM((sections, 2, rank_columns, width), jnp.bfloat16),
            pltpu.VMEM((sections + 1, rows, width), jnp.bfloat16),
            pltpu.VMEM((rows, width), jnp.bfloat16),
            pltpu.VMEM(records, jnp.bfloat16),
            pltpu.VMEM(records, jnp.bfloat16),
            pltpu.SemaphoreType.DMA((4,)),
            pltpu.SemaphoreType.DMA((14,)),
            pltpu.SemaphoreType.DMA((14,)),
            pltpu.SemaphoreType.DMA((2, sections)),
            pltpu.SemaphoreType.DMA((2, sections)),
            pltpu.VMEM((pieces, slot_count * lanes, 128), jnp.bfloat16),
            pltpu.VMEM((pieces, slot_count * lanes, 128), jnp.bfloat16),
            pltpu.VMEM((pieces, lanes, 128), jnp.bfloat16),
            pltpu.SemaphoreType.DMA((2, pieces)),
            pltpu.SemaphoreType.DMA((2, pieces)),
            pltpu.VMEM((2, rows, width + 128), jnp.bfloat16),
            pltpu.SemaphoreType.DMA((2,)),
            pltpu.SemaphoreType.DMA((2,)),
        ],
        compiler_params=pltpu.CompilerParams(
            collective_id=0, has_side_effects=True, vmem_limit_bytes=56 * 1024 * 1024
        ),
    )(inputs, cotangent, slot, down_weight, up_weight, select)


def body(
    inputs,
    cotangent,
    row_adapter_slot,
    deployed_adapter_ids,
    adapter_owner_device,
    adapter_down_weight,
    adapter_up_weight,
):
    section_index = lax.axis_index("section")
    pieces = lax.axis_size("dp")
    micro_count, row_count, width = inputs.shape
    slot_count = adapter_down_weight.shape[3]
    rank = adapter_down_weight.shape[4]
    rank_columns = slot_count * rank
    down_weight = adapter_down_weight.reshape(rank_columns, width)
    up_weight = adapter_up_weight.reshape(rank_columns, width)
    slot = lax.dynamic_index_in_dim(row_adapter_slot, section_index, 0, keepdims=False)
    adapter_ids = jnp.arange(adapter_owner_device.shape[0], dtype=jnp.int32)
    owner_of = jnp.sum(
        jnp.where(deployed_adapter_ids[..., None] == adapter_ids, adapter_owner_device, 0), axis=-1
    )
    owner_ids = jnp.arange(pieces, dtype=jnp.int32)
    select = (owner_of.T[:, None, :] == owner_ids[None, :, None]).astype(jnp.bfloat16)
    final = relay(inputs, cotangent, slot[:, None], down_weight, up_weight, select)
    final = final.reshape(2, 1, 1, 1, rank, width).astype(jnp.float32)
    return (final[0], final[1])


def solution(mesh):
    placed = (
        P(None, "dp", None),
        P(None, "dp", None),
        P(None, "dp"),
        P(),
        P(),
        P("section", None, "dp", None, None, None),
        P("section", None, "dp", None, None, None),
    )
    return jax.shard_map(
        body,
        mesh=mesh,
        in_specs=placed,
        out_specs=(P("section", None, "dp", None, None), P("section", None, "dp", None, None)),
        check_vma=False,
    )
```

```python
import jax
import jax.numpy as jnp
from jax import lax
from jax.experimental import pallas as pl
from jax.experimental.pallas import tpu as pltpu
from jax.sharding import PartitionSpec as P

adapter_scale = 0.5
epsilon = 1e-06


MESH = pl.DeviceIdType.MESH


def relay_kernel(
    inputs_ref,
    cotangent_ref,
    slot_ref,
    down_ref,
    up_ref,
    select_ref,
    grad_down_ref,
    grad_up_ref,
    normed_ref,
    grads_ref,
    weights,
    hidden_ref,
    grad_ref,
    normed_out,
    grads_out,
    own_sem,
    gather_send,
    gather_recv,
    rows_send,
    rows_recv,
    tiles_ref,
    pieces_in,
    owned,
    out_ref,
    send_sem,
    recv_sem,
):
    sections, unused_pair, rank_columns, width = weights.shape
    rows = inputs_ref.shape[1]
    half = rank_columns // 2
    me = lax.axis_index("section")
    core = lax.rem(me, 2)
    partner = me + 1 - 2 * core
    right = lax.rem(me + 2, sections)
    left = lax.rem(me + sections - 2, sections)
    far = lax.rem(me + 4, sections)

    pieces = lax.axis_size("dp")
    slot_count = select_ref.shape[0]
    lanes = width // 128
    side = 8
    me_dp = lax.axis_index("dp")
    me_z, me_y = lax.div(me_dp, side), lax.rem(me_dp, side)

    turn = 1 - 2 * core

    def peer(step):
        offset = lax.rem(step * 29, pieces)
        z = lax.rem(me_z + turn * lax.div(offset, side) + side, side)
        y = lax.rem(me_y + turn * lax.rem(offset, side) + side, side)
        return z * side + y

    barrier = pltpu.get_barrier_semaphore()
    for step in range(1, sections):
        pl.semaphore_signal(
            barrier,
            inc=1,
            device_id={"section": lax.rem(me + step, sections)},
            device_id_type=MESH,
        )

    def greet(step, carried):
        pl.semaphore_signal(
            barrier, inc=1, device_id={"dp": peer(step)}, device_id_type=MESH
        )
        return carried

    lax.fori_loop(1, pieces, greet, 0)
    pl.semaphore_wait(barrier, sections - 1 + pieces - 1)

    def pass_on(number, src, owner, which, target):
        return pltpu.make_async_remote_copy(
            src_ref=src,
            dst_ref=weights.at[owner, which],
            send_sem=gather_send.at[number],
            recv_sem=gather_recv.at[number],
            device_id={"section": target},
            device_id_type=MESH,
        )

    def forwarded(number, owner, which, target):
        return pass_on(number, weights.at[owner, which], owner, which, target)

    copies = [
        pass_on(0, down_ref, me, 0, right),
        pass_on(1, up_ref, me, 1, left),
        pass_on(2, up_ref, me, 1, right),
        pass_on(3, down_ref, me, 0, left),
        pass_on(4, down_ref, me, 0, partner),
        pass_on(5, up_ref, me, 1, partner),
    ]
    for copy in copies:
        copy.start()
    own = [
        pltpu.make_async_copy(down_ref, weights.at[me, 0], own_sem.at[0]),
        pltpu.make_async_copy(up_ref, weights.at[me, 1], own_sem.at[1]),
        pltpu.make_async_copy(inputs_ref.at[me], hidden_ref.at[0], own_sem.at[2]),
        pltpu.make_async_copy(cotangent_ref.at[me], grad_ref, own_sem.at[3]),
    ]
    for copy in own:
        copy.start()

    def send_on(number, owner, which, target):
        copy = forwarded(number, owner, which, target)
        copy.start()
        copies.append(copy)

    copies[0].wait_recv()
    send_on(6, left, 0, right)
    send_on(8, left, 0, partner)
    copies[1].wait_recv()
    send_on(7, right, 1, left)
    send_on(9, right, 1, partner)
    copies[2].wait_recv()
    send_on(10, left, 1, partner)
    copies[3].wait_recv()
    send_on(11, right, 0, partner)
    copies[6].wait_recv()
    send_on(12, far, 0, partner)
    copies[8].wait_recv()
    send_on(13, far, 1, partner)

    column_slot = lax.broadcasted_iota(jnp.int32, (rows, rank_columns), 1) // half
    row_mask = slot_ref[...] == column_slot
    for copy in own:
        copy.wait()
    for place in (4, 5, 7, 9, 10, 11, 12, 13):
        copies[place].wait_recv()

    def rows_copy(kind, section, place):
        source, target = ((normed_out, normed_ref), (grads_out, grads_ref))[kind]
        return pltpu.make_async_remote_copy(
            src_ref=source.at[section],
            dst_ref=target.at[place],
            send_sem=rows_send.at[kind, section],
            recv_sem=rows_recv.at[kind, place],
            device_id={"section": section},
            device_id_type=MESH,
        )

    def send_rows(kind, section):
        @pl.when(section != me)
        def start():
            rows_copy(kind, section, me).start()

    def norm_parts(section):
        hidden = hidden_ref[section].astype(jnp.float32)
        inverse = lax.rsqrt(jnp.mean(hidden * hidden, axis=-1, keepdims=True) + epsilon)
        return hidden, inverse, hidden * inverse

    def forward(section, carried):
        hidden, inverse, unit = norm_parts(section)
        normed = unit.astype(jnp.bfloat16)
        normed_out[section, :, 0:width] = normed
        rank = lax.dot_general(
            normed,
            weights[section, 0],
            (((1,), (1,)), ((), ())),
            preferred_element_type=jnp.float32,
        )
        rank = jnp.where(row_mask, rank, 0.0).astype(jnp.bfloat16)
        normed_out[section, :, width : width + rank_columns] = rank
        update = jnp.dot(rank, weights[section, 1], preferred_element_type=jnp.float32)
        hidden_ref[section + 1] = (hidden + adapter_scale * update).astype(jnp.bfloat16)

        @pl.when(section > 0)
        def send_last():
            send_rows(0, section - 1)

        return carried

    lax.fori_loop(0, sections, forward, 0)

    def backward(step, carried):
        section = sections - 1 - step
        hidden, inverse, unit = norm_parts(section)
        grads = grad_ref[...]
        grads_out[section, :, 0:width] = grads
        rank_grads = adapter_scale * lax.dot_general(
            grads,
            weights[section, 1],
            (((1,), (1,)), ((), ())),
            preferred_element_type=jnp.float32,
        )
        rank_grads = jnp.where(row_mask, rank_grads, 0.0).astype(jnp.bfloat16)
        grads_out[section, :, width : width + rank_columns] = rank_grads
        unit_grads = jnp.dot(
            rank_grads, weights[section, 0], preferred_element_type=jnp.float32
        )
        back = grads.astype(jnp.float32) + inverse * (
            unit_grads - unit * jnp.mean(unit_grads * unit, axis=-1, keepdims=True)
        )
        grad_ref[...] = back.astype(jnp.bfloat16)

        @pl.when(step == 0)
        def send_top():
            send_rows(0, sections - 1)

        @pl.when(step > 0)
        def send_last():
            send_rows(1, section + 1)

        return carried

    lax.fori_loop(0, sections, backward, 0)
    normed_ref[me] = normed_out[me]
    grads_ref[me] = grads_out[me]
    send_rows(1, 0)
    for copy in copies:
        copy.wait_send()

    def finish(step, carried):
        other = lax.rem(me + step, sections)
        for kind in range(2):
            copy = rows_copy(kind, other, other)
            copy.wait_send()
            copy.wait_recv()
        return carried

    lax.fori_loop(1, sections, finish, 0)

    tiles = []
    for rank_from, rows_from in ((grads_ref, normed_ref), (normed_ref, grads_ref)):
        rank_values = rank_from[:, :, width : width + rank_columns].reshape(-1, rank_columns)
        row_values = rows_from[:, :, 0:width].reshape(-1, width)
        tile = lax.dot_general(
            rank_values,
            row_values,
            (((0,), (0,)), ((), ())),
            preferred_element_type=jnp.float32,
        )
        if rank_from is normed_ref:
            tile = adapter_scale * tile
        tile = tile.astype(jnp.bfloat16)
        blocks = [
            tile[k * half : (k + 1) * half, 128 * lane : 128 * (lane + 1)]
            for k in range(slot_count)
            for lane in range(lanes)
        ]
        tiles.append(jnp.swapaxes(jnp.stack(blocks), 0, 1))
    tiles_ref[0:half] = tiles[0]
    tiles_ref[half : 2 * half] = tiles[1]

    def piece_copy(stage, other, place):
        source, target = ((tiles_ref, pieces_in), (owned, out_ref))[stage]
        return pltpu.make_async_remote_copy(
            src_ref=source.at[other],
            dst_ref=target.at[place],
            send_sem=send_sem.at[stage, other],
            recv_sem=recv_sem.at[stage, place],
            device_id={"dp": other},
            device_id_type=MESH,
        )

    def send(stage):
        def one(step, carried):
            piece_copy(stage, peer(step), me_dp).start()
            return carried

        lax.fori_loop(1, pieces, one, 0)

    def receive(stage):
        def one(step, carried):
            other = peer(step)
            piece_copy(stage, other, other).wait_recv()
            return carried

        lax.fori_loop(1, pieces, one, 0)

    send(0)
    pieces_in[me_dp] = tiles_ref[me_dp]
    receive(0)
    by_lanes = jnp.swapaxes(pieces_in[...], 0, 1)
    sums = []
    for lane in range(lanes):
        total = None
        for k in range(slot_count):
            term = jnp.dot(
                select_ref[k], by_lanes[k * lanes + lane], preferred_element_type=jnp.float32
            )
            total = term if total is None else total + term
        sums.append(total.astype(jnp.bfloat16))
    owned[...] = jnp.swapaxes(jnp.stack(sums), 0, 1)
    send(1)
    out_ref[me_dp] = owned[me_dp]
    receive(1)
    last = jnp.swapaxes(out_ref[...], 0, 1)
    for lane in range(lanes):
        columns = slice(128 * lane, 128 * (lane + 1))
        grad_down_ref[:, columns] = last[lane, 0:half].astype(jnp.float32)
        grad_up_ref[:, columns] = last[lane, half : 2 * half].astype(jnp.float32)

    def drain(step, carried):
        other = peer(step)
        for stage in range(2):
            piece_copy(stage, other, other).wait_send()
        return carried

    lax.fori_loop(1, pieces, drain, 0)


def relay(inputs, cotangent, slot, down_weight, up_weight, select):
    sections = lax.axis_size("section")
    pieces = lax.axis_size("dp")
    rank_columns, width = down_weight.shape
    rows = inputs.shape[1]
    slot_count = select.shape[0]
    lanes = width // 128
    vmem = pl.BlockSpec(memory_space=pltpu.VMEM)
    anywhere = pl.BlockSpec(memory_space=pl.ANY)
    records = (sections, rows, width + 128)
    return pl.pallas_call(
        relay_kernel,
        out_shape=[jax.ShapeDtypeStruct((pieces // 2, width), jnp.float32)] * 2,
        in_specs=[anywhere, anywhere, vmem, anywhere, anywhere, vmem],
        out_specs=[vmem] * 2,
        scratch_shapes=[
            pltpu.VMEM(records, jnp.bfloat16),
            pltpu.VMEM(records, jnp.bfloat16),
            pltpu.VMEM((sections, 2, rank_columns, width), jnp.bfloat16),
            pltpu.VMEM((sections + 1, rows, width), jnp.bfloat16),
            pltpu.VMEM((rows, width), jnp.bfloat16),
            pltpu.VMEM(records, jnp.bfloat16),
            pltpu.VMEM(records, jnp.bfloat16),
            pltpu.SemaphoreType.DMA((4,)),
            pltpu.SemaphoreType.DMA((14,)),
            pltpu.SemaphoreType.DMA((14,)),
            pltpu.SemaphoreType.DMA((2, sections)),
            pltpu.SemaphoreType.DMA((2, sections)),
            pltpu.VMEM((pieces, slot_count * lanes, 128), jnp.bfloat16),
            pltpu.VMEM((pieces, slot_count * lanes, 128), jnp.bfloat16),
            pltpu.VMEM((pieces, lanes, 128), jnp.bfloat16),
            pltpu.VMEM((pieces, lanes, 128), jnp.bfloat16),
            pltpu.SemaphoreType.DMA((2, pieces)),
            pltpu.SemaphoreType.DMA((2, pieces)),
        ],
        compiler_params=pltpu.CompilerParams(
            collective_id=0, has_side_effects=True, vmem_limit_bytes=56 * 1024 * 1024
        ),
    )(inputs, cotangent, slot, down_weight, up_weight, select)


def body(
    inputs,
    cotangent,
    row_adapter_slot,
    deployed_adapter_ids,
    adapter_owner_device,
    adapter_down_weight,
    adapter_up_weight,
):
    section_index = lax.axis_index("section")
    pieces = lax.axis_size("dp")
    micro_count, row_count, width = inputs.shape
    slot_count = adapter_down_weight.shape[3]
    rank = adapter_down_weight.shape[4]
    rank_columns = slot_count * rank
    down_weight = adapter_down_weight.reshape(rank_columns, width)
    up_weight = adapter_up_weight.reshape(rank_columns, width)
    slot = lax.dynamic_index_in_dim(row_adapter_slot, section_index, 0, keepdims=False)
    adapter_ids = jnp.arange(adapter_owner_device.shape[0], dtype=jnp.int32)
    owner_of = jnp.sum(
        jnp.where(deployed_adapter_ids[..., None] == adapter_ids, adapter_owner_device, 0), axis=-1
    )
    owner_ids = jnp.arange(pieces, dtype=jnp.int32)
    select = (owner_of.T[:, None, :] == owner_ids[None, :, None]).astype(jnp.bfloat16)
    grad_down, grad_up = relay(inputs, cotangent, slot[:, None], down_weight, up_weight, select)
    return (
        grad_down.reshape(1, 1, 1, rank, width),
        grad_up.reshape(1, 1, 1, rank, width),
    )


def solution(mesh):
    placed = (
        P(None, "dp", None),
        P(None, "dp", None),
        P(None, "dp"),
        P(),
        P(),
        P("section", None, "dp", None, None, None),
        P("section", None, "dp", None, None, None),
    )
    return jax.shard_map(
        body,
        mesh=mesh,
        in_specs=placed,
        out_specs=(P("section", None, "dp", None, None), P("section", None, "dp", None, None)),
        check_vma=False,
    )
```
